256 devices in a mesh: wide: 64 (over x, z, y_hi), narrow: 4 (over y_lo, core).
Axes of the slice: x: 4, y: 4 (y_hi: 2, y_lo: 2; y = y_hi * 2 + y_lo), z: 8, core: 2. Of those that a mesh axis runs over, the one named last changes fastest.
Arguments:
- latent: bfloat16 [64, 32, 48, 256], P('wide', 'narrow'), may hold values from -12 to 12
- conv_first: bfloat16 [6912, 256], P(None, 'wide'), may hold values from -0.078125 to 0.078125
- conv_second: bfloat16 [6912, 256], P(None, 'wide'), may hold values from -0.078125 to 0.078125
- embed_weight: bfloat16 [1024, 2240], P(None, 'wide'), may hold values from -0.1875 to 0.1875
- qkv_weight: bfloat16 [3, 2240, 2240], P(None, None, 'narrow'), may hold values from -0.125 to 0.125
Outputs:
- mixed: bfloat16 [24576, 2240], P('wide', 'narrow')
The draws below stay inside these ranges and needn't reach their ends.
All inputs are finite; a program needn't handle non-finite values.
Results may differ from the reference program's by a relative error of at most 0.011.
Values may be sent and summed in bfloat16 or wider, within the bound.
No kernel may reach another device: no remote copies, remote signals or barrier semaphores. Data moves between devices by JAX's collectives and lax.ppermute only.
A program may use at most 128 MiB of HBM per device.

```python
import jax
import jax.numpy as jnp
from jax import lax

C = 256
HEADS = 20
HEAD_DIM = 112
LAT_W = 48
D = 2240
H = 32
FRAMES = 64


def draw_latent(key, part):
    noise_key, common_key, frame_key = jax.random.split(jax.random.fold_in(key, 17), 3)
    full_shape = (FRAMES, H, LAT_W, C)
    noise_part = jax.random.normal(noise_key, full_shape, jnp.float32)
    common = jax.random.normal(common_key, (1, 1, 1, C), jnp.float32)
    per_frame = 0.7 * jax.random.normal(frame_key, (FRAMES, 1, 1, C), jnp.float32)
    return jnp.clip(noise_part + common + per_frame, -12.0, 12.0).astype(jnp.bfloat16)


def block_levels(own_key, dims, cuts, smallest, high):
    def one(position, parts):
        steps = jax.random.uniform(jax.random.fold_in(jax.random.fold_in(own_key, 6), position), (parts,), jnp.float32, smallest / len(cuts), high / len(cuts))
        return jnp.repeat(jnp.exp(steps), dims[position] // parts).reshape((-1,) + (1,) * (len(dims) - position - 1))

    level = one(*cuts[0])
    for cut in cuts[1:]:
        level = level * one(*cut)
    return level


def scatter_about(stream_key, extent, scale, reach, cuts=(), dtype=jnp.bfloat16):
    array = scale * jax.random.normal(stream_key, extent, jnp.float32)
    if cuts:
        array = array * block_levels(stream_key, extent, cuts, -0.22, 0.18)
    return jnp.clip(array, -reach, reach).astype(dtype)


def setup_inputs(seed: int = 0) -> dict:
    keys = jax.random.split(jax.random.key(seed), 6)
    latent = draw_latent(jax.random.fold_in(keys[5], 71), 0)
    conv_first = scatter_about(keys[1], (27 * C, C), (27 * C) ** -0.5, 0.078125, ((1, 64),))
    conv_second = scatter_about(keys[2], (27 * C, C), (27 * C) ** -0.5, 0.078125, ((1, 64),))
    embed_weight = scatter_about(keys[3], (4 * C, D), (4 * C) ** -0.5, 0.1875, ((1, 64),))
    qkv_weight = scatter_about(keys[4], (3, D, D), D ** -0.5, 0.125, ((2, 4),))
    return {"latent": latent, "conv_first": conv_first, "conv_second": conv_second, "embed_weight": embed_weight, "qkv_weight": qkv_weight}


def causal_conv(volume, weight):
    frame_count, row_count, col_count, chan_count = volume.shape
    padded = jnp.pad(volume, ((2, 0), (1, 1), (1, 1), (0, 0)))
    summed = jnp.zeros((frame_count * row_count * col_count, weight.shape[1]), jnp.float32)
    for kernel_tap in range(27):
        time_step = kernel_tap // 9
        row_step = (kernel_tap // 3) % 3
        col_step = kernel_tap % 3
        window = padded[time_step:time_step + frame_count, row_step:row_step + row_count, col_step:col_step + col_count]
        window = window.reshape(-1, chan_count)
        summed = summed + jnp.dot(window, weight[kernel_tap * chan_count:(kernel_tap + 1) * chan_count], preferred_element_type=jnp.float32)
    return summed


def frame_step(carry, inputs):
    state, key_total = carry
    query_feat, key_feat, val_rows = inputs
    token_count = query_feat.shape[0]
    query_wide = query_feat.astype(jnp.float32)
    key_wide = key_feat.astype(jnp.float32)
    val_wide = val_rows.astype(jnp.float32)
    scores = jnp.einsum("thd,shd->hts", query_wide, key_wide, precision=lax.Precision.HIGHEST)
    order_ids = jnp.arange(token_count)
    allowed = order_ids[None, :] <= order_ids[:, None]
    scores = jnp.where(allowed[None], scores, 0.0)
    local_den = jnp.sum(scores, axis=-1)
    weight_low = scores.astype(jnp.bfloat16).astype(jnp.float32)
    local_num = jnp.einsum("hts,she->the", weight_low, val_wide, precision=lax.Precision.HIGHEST)
    carried_num = jnp.einsum("thd,hde->the", query_wide, state, precision=lax.Precision.HIGHEST)
    carried_den = jnp.einsum("thd,hd->th", query_wide, key_total, precision=lax.Precision.HIGHEST)
    result = (local_num + carried_num) / (local_den.T + carried_den)[..., None]
    new_state = state + jnp.einsum("thd,the->hde", key_wide, val_wide, precision=lax.Precision.HIGHEST)
    new_total = key_total + jnp.sum(key_wide, axis=0)
    return (new_state, new_total), result.astype(jnp.bfloat16).reshape(token_count, -1)


def reference(latent, conv_first, conv_second, embed_weight, qkv_weight):
    frame_count, row_count, col_count, chan_count = latent.shape
    first = causal_conv(latent, conv_first)
    activated = jax.nn.silu(first).astype(jnp.bfloat16).reshape(latent.shape)
    second = causal_conv(activated, conv_second) + latent.reshape(-1, chan_count).astype(jnp.float32)
    block_out = second.astype(jnp.bfloat16)
    patches = block_out.reshape(frame_count, row_count // 2, 2, col_count // 2, 2, chan_count)
    patches = patches.transpose(0, 1, 3, 2, 4, 5).reshape(-1, 4 * chan_count)
    embedded = jnp.dot(patches, embed_weight, preferred_element_type=jnp.float32).astype(jnp.bfloat16)
    projected = [jnp.dot(embedded, qkv_weight[which_part], preferred_element_type=jnp.float32).astype(jnp.bfloat16) for which_part in range(3)]
    query_feat = (jax.nn.elu(projected[0].astype(jnp.float32)) + 1.0).astype(jnp.bfloat16)
    key_feat = (jax.nn.elu(projected[1].astype(jnp.float32)) + 1.0).astype(jnp.bfloat16)
    head_shape = (frame_count, -1, HEADS, HEAD_DIM)
    initial = (jnp.zeros((HEADS, HEAD_DIM, HEAD_DIM), jnp.float32), jnp.zeros((HEADS, HEAD_DIM), jnp.float32))
    final_carry, mixed = lax.scan(frame_step, initial, (query_feat.reshape(head_shape), key_feat.reshape(head_shape), projected[2].reshape(head_shape)))
    return mixed.reshape(-1, HEADS * HEAD_DIM)
```

```python
import jax
import jax.numpy as jnp
from jax import lax
from jax.experimental import pallas as pl
from jax.experimental.pallas import tpu as pltpu
from jax.sharding import PartitionSpec as P

HEAD_DIM = 112
NX, NZ, NY = 4, 8, 2
BF16 = jnp.bfloat16
F32 = jnp.float32


def wide_index(x, z, y):
    return (x * NZ + z) * NY + y


ALONG_Z = [
    [wide_index(x, z, y) for z in range(NZ)] for x in range(NX) for y in range(NY)
]
ALONG_XY = [
    [wide_index(x, z, y) for x in range(NX) for y in range(NY)] for z in range(NZ)
]


def delayed(x, by):
    size = lax.axis_size("wide")
    return lax.ppermute(x, "wide", [(i, i + by) for i in range(size - by)])


def other(x, mask):
    return lax.ppermute(x, "narrow", [(i, i ^ mask) for i in range(4)])


def spread(x, groups):
    count = len(groups[0])
    copies = jnp.broadcast_to(x[None], (count,) + x.shape)
    return lax.all_to_all(copies, "wide", 0, 0, axis_index_groups=groups, tiled=True)


def gather_wide(shard):
    by_z = spread(shard, ALONG_Z)
    by_xy = spread(by_z, ALONG_XY)
    blocks = by_xy.reshape((NX, NY, NZ) + shard.shape)
    return jnp.moveaxis(blocks, 1, 2).reshape((NX * NY * NZ,) + shard.shape)


def dot_nt(a, b):
    return lax.dot_general(a, b, (((1,), (1,)), ((), ())), preferred_element_type=F32)


def column_sum(prod_ref, rows, cols, width):
    col = lax.broadcasted_iota(jnp.int32, (rows, 1), 0) % cols
    left = prod_ref[7 : 7 + rows, :width]
    mid = prod_ref[8 : 8 + rows, width : 2 * width]
    right = prod_ref[9 : 9 + rows, 2 * width : 3 * width]
    return jnp.where(col != 0, left, 0.0) + mid + jnp.where(col != cols - 1, right, 0.0)


def first_conv_kernel(cols, x_ref, w_ref, o_ref, pad_ref, tap_ref, prod_ref):
    tokens = x_ref.shape[1]
    width = w_ref.shape[0]
    pad_ref[:, :cols, :] = jnp.zeros((3, cols, 256), BF16)
    pad_ref[:, cols + tokens :, :] = jnp.zeros((3, cols, 256), BF16)
    pad_ref[:, cols : cols + tokens, :] = x_ref[...]
    for tap in range(27):
        tap_ref[tap // 3, tap % 3 * width : (tap % 3 + 1) * width, :] = w_ref[
            :, tap * 256 : (tap + 1) * 256
        ]
    prod_ref[0:8, :] = jnp.zeros((8, 3 * width), F32)
    prod_ref[8 + tokens :, :] = jnp.zeros((8, 3 * width), F32)
    chunk = tokens // 4
    for part in range(4):
        total = jnp.zeros((chunk, 3 * width), F32)
        for tap in range(9):
            start = part * chunk + tap % 3 * cols
            total += dot_nt(pad_ref[tap // 3, start : start + chunk, :], tap_ref[tap])
        prod_ref[8 + part * chunk : 8 + (part + 1) * chunk, :] = total
    first = column_sum(prod_ref, tokens, cols, width)
    o_ref[...] = (first / (1.0 + jnp.exp(-first))).astype(BF16)


def first_conv(frames, weight, cols):
    tokens = frames.shape[1]
    width = weight.shape[0]

    def kernel(*refs):
        first_conv_kernel(cols, *refs)

    return pl.pallas_call(
        kernel,
        out_shape=jax.ShapeDtypeStruct((tokens, width), BF16),
        in_specs=[pl.BlockSpec(memory_space=pltpu.VMEM)] * 2,
        out_specs=pl.BlockSpec(memory_space=pltpu.VMEM),
        scratch_shapes=[
            pltpu.VMEM((3, tokens + 2 * cols, 256), BF16),
            pltpu.VMEM((9, 3 * width, 256), BF16),
            pltpu.VMEM((tokens + 16, 3 * width), F32),
        ],
        name="first_conv",
    )(frames, weight)


def second_conv_kernel(
    cols, side_ref, a2_ref, a1_ref, a0_ref, w_ref, keep_ref, send_ref, pad_ref, tap_ref, prod_ref
):
    tokens, chans = a0_ref.shape
    depth = 3 * chans
    width = w_ref.shape[0]
    half = tokens // 2
    pad_ref[:cols, :] = jnp.zeros((cols, depth), BF16)
    pad_ref[cols + tokens :, :] = jnp.zeros((cols, depth), BF16)
    pad_ref[cols : cols + tokens, :] = jnp.concatenate(
        [a2_ref[...], a1_ref[...], a0_ref[...]], axis=1
    )
    for tap in range(9):
        tap_ref[tap // 3, tap % 3 * width : (tap % 3 + 1) * width, :] = w_ref[
            :, tap * depth : (tap + 1) * depth
        ]
    prod_ref[0:8, :] = jnp.zeros((8, 3 * width), F32)
    prod_ref[8 + tokens :, :] = jnp.zeros((8, 3 * width), F32)
    chunk = tokens // 8
    for part in range(8):
        total = jnp.zeros((chunk, 3 * width), F32)
        for tap in range(3):
            start = part * chunk + tap * cols
            total += dot_nt(pad_ref[start : start + chunk, :], tap_ref[tap])
        prod_ref[8 + part * chunk : 8 + (part + 1) * chunk, :] = total
    summed = column_sum(prod_ref, tokens, cols, width)

    @pl.when(side_ref[0] == 0)
    def _():
        keep_ref[...] = summed[:half]
        send_ref[...] = summed[half:].astype(BF16)

    @pl.when(side_ref[0] == 1)
    def _():
        keep_ref[...] = summed[half:]
        send_ref[...] = summed[:half].astype(BF16)


def second_conv(side, a2, a1, a0, weight, cols):
    tokens, chans = a0.shape
    width = weight.shape[0]

    def kernel(*refs):
        second_conv_kernel(cols, *refs)

    return pl.pallas_call(
        kernel,
        out_shape=(
            jax.ShapeDtypeStruct((tokens // 2, width), F32),
            jax.ShapeDtypeStruct((tokens // 2, width), BF16),
        ),
        in_specs=[pl.BlockSpec(memory_space=pltpu.SMEM)]
        + [pl.BlockSpec(memory_space=pltpu.VMEM)] * 4,
        out_specs=(
            pl.BlockSpec(memory_space=pltpu.VMEM),
            pl.BlockSpec(memory_space=pltpu.VMEM),
        ),
        scratch_shapes=[
            pltpu.VMEM((tokens + 2 * cols, 3 * chans), BF16),
            pltpu.VMEM((3, 3 * width, 3 * chans), BF16),
            pltpu.VMEM((tokens + 16, 3 * width), F32),
        ],
        name="second_conv",
    )(side, a2, a1, a0, weight)


def whole_frames(latent):
    me = lax.axis_index("narrow")
    strip = jnp.concatenate([delayed(latent, 2), delayed(latent, 1), latent], axis=0)
    far = other(strip, 2)
    near = other(jnp.stack([strip, far]), 1)
    pieces = jnp.stack([strip, near[0], far, near[1]])
    ordered = [lax.dynamic_index_in_dim(pieces, me ^ k, 0, keepdims=False) for k in range(4)]
    frames = jnp.concatenate(ordered, axis=1)
    return frames.reshape(3, -1, latent.shape[3])


def own_column(weight, index):
    return lax.dynamic_index_in_dim(weight.T, index, 0, keepdims=False)


def per_device(latent, conv_first, conv_second, embed_weight, qkv_weight):
    row_count = latent.shape[1]
    col_count = latent.shape[2]
    chan_count = latent.shape[3]
    lane_count = 4
    me = lax.axis_index("narrow")
    core = me % 2
    chans_here = chan_count // lane_count

    first_shard = own_column(conv_first, me).reshape(-1, 128)
    first_weight = gather_wide(first_shard).reshape(chans_here, -1)

    pick = (
        lax.broadcasted_iota(jnp.int32, (chan_count, chans_here), 0)
        == lane_count * lax.broadcasted_iota(jnp.int32, (chan_count, chans_here), 1) + me
    ).astype(BF16)
    second_shard = jnp.dot(
        conv_second.T.reshape(-1, chan_count), pick, preferred_element_type=F32
    ).astype(BF16)
    second_shard = second_shard.reshape(lane_count, 3, 9, chans_here)
    second_shard = jnp.moveaxis(second_shard, 1, 2).reshape(-1, 128)
    second_weight = gather_wide(second_shard).reshape(chan_count, -1)

    quarter = embed_weight.shape[0] // 4
    embed_shard = lax.dynamic_slice_in_dim(embed_weight.T, me * quarter, quarter, axis=1)
    embed_mine = gather_wide(embed_shard.reshape(-1, 128)).reshape(-1, quarter)
    embed_pair = jnp.stack([embed_mine, other(embed_mine, 2)])
    embed_near = other(embed_pair, 1)
    embed_all = jnp.stack([embed_pair[0], embed_near[0], embed_pair[1], embed_near[1]])
    embed_all = [
        lax.dynamic_index_in_dim(embed_all, me ^ k, 0, keepdims=False) for k in range(4)
    ]

    frames = whole_frames(latent)
    activated = first_conv(frames, first_weight, col_count)
    keep, send = second_conv(
        core.astype(jnp.int32).reshape(1),
        delayed(activated, 2),
        delayed(activated, 1),
        activated,
        second_weight,
        col_count,
    )
    half = keep.shape[0]
    chip_sum = keep + other(send, 1).astype(F32)
    residual = lax.dynamic_slice_in_dim(frames[2], core * half, half, axis=0)
    block_out = chip_sum + other(chip_sum.astype(BF16), 2).astype(F32) + residual.astype(F32)
    block_out = block_out.astype(BF16)
    half_rows = half // col_count
    patches = block_out.reshape(half_rows // 2, 2, col_count // 2, 2, chan_count)
    patches = patches.transpose(0, 2, 1, 3, 4).reshape(-1, 4 * chan_count)
    near_patches = other(patches, 1)
    whole_patches = jnp.concatenate(
        [
            jnp.where(core == 0, patches, near_patches),
            jnp.where(core == 0, near_patches, patches),
        ],
        axis=0,
    )
    embedded = sum(
        dot_nt(whole_patches[:, k * quarter : (k + 1) * quarter], embed_all[k]) for k in range(4)
    ).astype(BF16)

    heads_here = qkv_weight.shape[2] // HEAD_DIM
    token_count = embedded.shape[0]
    key_raw = jnp.dot(embedded, qkv_weight[1], preferred_element_type=F32).astype(BF16).astype(F32)
    val_rows = jnp.dot(embedded, qkv_weight[2], preferred_element_type=F32).astype(BF16)
    query_raw = (
        jnp.dot(embedded, qkv_weight[0], preferred_element_type=F32).astype(BF16).astype(F32)
    )
    query_feat = (
        (jax.nn.elu(query_raw) + 1.0).astype(BF16).reshape(token_count, heads_here, HEAD_DIM)
    )
    key_feat = (jax.nn.elu(key_raw) + 1.0).astype(BF16).reshape(token_count, heads_here, HEAD_DIM)
    val_heads = val_rows.reshape(token_count, heads_here, HEAD_DIM)
    scores = jnp.einsum("thd,shd->hts", query_feat, key_feat, preferred_element_type=F32)
    row_ids = lax.broadcasted_iota(jnp.int32, (token_count, token_count), 0)
    col_ids = lax.broadcasted_iota(jnp.int32, (token_count, token_count), 1)
    scores = jnp.where((col_ids <= row_ids)[None], scores, 0.0)
    local_den = jnp.sum(scores, axis=-1)
    local_num = jnp.einsum(
        "hts,she->the", scores.astype(BF16), val_heads, preferred_element_type=F32
    )
    state_local = jnp.einsum("thd,the->hde", key_feat, val_heads, preferred_element_type=F32)
    key_local = jnp.sum(key_feat, axis=0, dtype=F32)
    flat_state = jnp.concatenate([state_local.reshape(-1), key_local.reshape(-1)])
    length_all = flat_state.shape[0]
    peer_count = lax.axis_size("wide")
    per_peer = -(-length_all // peer_count)
    piece_grid = jnp.pad(flat_state, (0, per_peer * peer_count - length_all)).reshape(
        peer_count, per_peer
    )
    lower_ones = (
        lax.broadcasted_iota(jnp.int32, (peer_count, peer_count), 1)
        < lax.broadcasted_iota(jnp.int32, (peer_count, peer_count), 0)
    ).astype(F32)
    arrived = lax.all_to_all(
        piece_grid.astype(BF16), "wide", split_axis=0, concat_axis=0, tiled=True
    )
    partial_sums = jnp.dot(lower_ones, arrived.astype(F32), precision=lax.Precision.HIGHEST)
    spread_back = lax.all_to_all(
        partial_sums.astype(BF16), "wide", split_axis=0, concat_axis=0, tiled=True
    ).astype(F32)
    flat_prefix = spread_back.reshape(-1)[:length_all]
    state_size = state_local.size
    state_prev = flat_prefix[:state_size].reshape(state_local.shape)
    key_prev = flat_prefix[state_size:].reshape(key_local.shape)
    query_wide = query_feat.astype(F32)
    carried_num = jnp.einsum(
        "thd,hde->the", query_wide, state_prev, precision=lax.Precision.HIGHEST
    )
    carried_den = jnp.einsum("thd,hd->th", query_wide, key_prev, precision=lax.Precision.HIGHEST)
    result = (local_num + carried_num) / (local_den.T + carried_den)[..., None]
    return result.astype(BF16).reshape(token_count, heads_here * HEAD_DIM)


def solution(mesh):
    return jax.shard_map(
        per_device,
        mesh=mesh,
        in_specs=(
            P("wide", "narrow", None, None),
            P(None, "wide"),
            P(None, "wide"),
            P(None, "wide"),
            P(None, None, "narrow"),
        ),
        out_specs=P("wide", "narrow"),
        check_vma=False,
    )
```

```python
import jax
import jax.numpy as jnp
from jax import lax
from jax.experimental import pallas as pl
from jax.experimental.pallas import tpu as pltpu
from jax.sharding import PartitionSpec as P


HEAD_DIM = 112
NX, NZ, NY = 4, 8, 2
BOTH = ("wide", "narrow")
BF16 = jnp.bfloat16
F32 = jnp.float32


def wide_index(x, z, y):
    return (x * NZ + z) * NY + y


ALONG_Z = [
    [wide_index(x, z, y) for z in range(NZ)] for x in range(NX) for y in range(NY)
]
ALONG_XY = [
    [wide_index(x, z, y) * 4 + (role ^ 2 * y) for x in range(NX) for y in range(NY)]
    for z in range(NZ)
    for role in range(4)
]


def delayed(x, by):
    size = lax.axis_size("wide")
    pairs = [
        (4 * i + n, 4 * (i + by) + (n ^ 2 * (by % 2))) for i in range(size - by) for n in range(4)
    ]
    return lax.ppermute(x, BOTH, pairs)


def other(x, mask):
    return lax.ppermute(x, "narrow", [(i, i ^ mask) for i in range(4)])


def spread(x, axis, groups):
    count = len(groups[0])
    copies = jnp.broadcast_to(x[None], (count,) + x.shape)
    return lax.all_to_all(copies, axis, 0, 0, axis_index_groups=groups, tiled=True)


def in_wide_order(by_xy, shape):
    blocks = by_xy.reshape((NX, NY, NZ) + shape)
    return jnp.moveaxis(blocks, 1, 2).reshape((NX * NY * NZ,) + shape)


def dot_nt(a, b):
    return lax.dot_general(a, b, (((1,), (1,)), ((), ())), preferred_element_type=F32)


def column_sum(prod_ref, rows, cols, width):
    col = lax.broadcasted_iota(jnp.int32, (rows, 1), 0) % cols
    left = prod_ref[7 : 7 + rows, :width]
    mid = prod_ref[8 : 8 + rows, width : 2 * width]
    right = prod_ref[9 : 9 + rows, 2 * width : 3 * width]
    return jnp.where(col != 0, left, 0.0) + mid + jnp.where(col != cols - 1, right, 0.0)


def first_conv_kernel(
    cols, me_ref, now0, now1, now2, now3, old0, old1, old2, old3, w_ref, o_ref, res_ref,
    pad_ref, tap_ref, prod_ref,
):
    strip = now0.shape[0]
    tokens = 4 * strip
    width = w_ref.shape[0]
    me = me_ref[0]
    pad_ref[:, :cols, :] = jnp.zeros((3, cols, 256), BF16)
    pad_ref[:, cols + tokens :, :] = jnp.zeros((3, cols, 256), BF16)
    for k, (now, old) in enumerate(((now0, old0), (now1, old1), (now2, old2), (now3, old3))):
        place = pl.ds(pl.multiple_of(cols + (me ^ k) * strip, 16), strip)
        pad_ref[2, place, :] = now[...]
        pad_ref[0, place, :] = old[0]
        place = pl.ds(pl.multiple_of(cols + (me ^ k ^ 2) * strip, 16), strip)
        pad_ref[1, place, :] = old[1]
    half = tokens // 2
    res_ref[...] = pad_ref[2, pl.ds(pl.multiple_of(cols + (me & 1) * half, 16), half), :]
    for tap in range(27):
        tap_ref[tap // 3, tap % 3 * width : (tap % 3 + 1) * width, :] = w_ref[
            :, tap * 256 : (tap + 1) * 256
        ]
    prod_ref[0:8, :] = jnp.zeros((8, 3 * width), F32)
    prod_ref[8 + tokens :, :] = jnp.zeros((8, 3 * width), F32)
    chunk = tokens // 4
    for part in range(4):
        total = jnp.zeros((chunk, 3 * width), F32)
        for tap in range(9):
            start = part * chunk + tap % 3 * cols
            total += dot_nt(pad_ref[tap // 3, start : start + chunk, :], tap_ref[tap])
        prod_ref[8 + part * chunk : 8 + (part + 1) * chunk, :] = total
    first = column_sum(prod_ref, tokens, cols, width)
    o_ref[...] = (first / (1.0 + jnp.exp(-first))).astype(BF16)


VMEM_SPEC = pl.BlockSpec(memory_space=pltpu.VMEM)
SMEM_SPEC = pl.BlockSpec(memory_space=pltpu.SMEM)


def first_conv(me, now, old, weight, cols):
    tokens = 4 * now[0].shape[0]
    width = weight.shape[0]

    def kernel(*refs):
        first_conv_kernel(cols, *refs)

    return pl.pallas_call(
        kernel,
        out_shape=(
            jax.ShapeDtypeStruct((tokens, width), BF16),
            jax.ShapeDtypeStruct((tokens // 2, 256), BF16),
        ),
        in_specs=[SMEM_SPEC] + [VMEM_SPEC] * 9,
        out_specs=(VMEM_SPEC, VMEM_SPEC),
        scratch_shapes=[
            pltpu.VMEM((3, tokens + 2 * cols, 256), BF16),
            pltpu.VMEM((9, 3 * width, 256), BF16),
            pltpu.VMEM((tokens + 16, 3 * width), F32),
        ],
        name="first_conv",
    )(me, *now, *old, weight)


def second_conv_kernel(
    cols, side_ref, a2_ref, a1_ref, a0_ref, w_ref, keep_ref, send_ref, pad_ref, tap_ref, prod_ref
):
    tokens, chans = a0_ref.shape
    depth = 3 * chans
    width = w_ref.shape[0]
    half = tokens // 2
    pad_ref[:cols, :] = jnp.zeros((cols, depth), BF16)
    pad_ref[cols + tokens :, :] = jnp.zeros((cols, depth), BF16)
    pad_ref[cols : cols + tokens, :] = jnp.concatenate(
        [a2_ref[...], a1_ref[...], a0_ref[...]], axis=1
    )
    for tap in range(9):
        tap_ref[tap // 3, tap % 3 * width : (tap % 3 + 1) * width, :] = w_ref[
            :, tap * depth : (tap + 1) * depth
        ]
    prod_ref[0:8, :] = jnp.zeros((8, 3 * width), F32)
    prod_ref[8 + tokens :, :] = jnp.zeros((8, 3 * width), F32)
    chunk = tokens // 8
    for part in range(8):
        total = jnp.zeros((chunk, 3 * width), F32)
        for tap in range(3):
            start = part * chunk + tap * cols
            total += dot_nt(pad_ref[start : start + chunk, :], tap_ref[tap])
        prod_ref[8 + part * chunk : 8 + (part + 1) * chunk, :] = total
    summed = column_sum(prod_ref, tokens, cols, width)

    @pl.when(side_ref[0] == 0)
    def _():
        keep_ref[...] = summed[:half]
        send_ref[...] = summed[half:].astype(BF16)

    @pl.when(side_ref[0] == 1)
    def _():
        keep_ref[...] = summed[half:]
        send_ref[...] = summed[:half].astype(BF16)


def second_conv(side, a2, a1, a0, weight, cols):
    tokens, chans = a0.shape
    width = weight.shape[0]

    def kernel(*refs):
        second_conv_kernel(cols, *refs)

    return pl.pallas_call(
        kernel,
        out_shape=(
            jax.ShapeDtypeStruct((tokens // 2, width), F32),
            jax.ShapeDtypeStruct((tokens // 2, width), BF16),
        ),
        in_specs=[SMEM_SPEC] + [VMEM_SPEC] * 4,
        out_specs=(VMEM_SPEC, VMEM_SPEC),
        scratch_shapes=[
            pltpu.VMEM((tokens + 2 * cols, 3 * chans), BF16),
            pltpu.VMEM((3, 3 * width, 3 * chans), BF16),
            pltpu.VMEM((tokens + 16, 3 * width), F32),
        ],
        name="second_conv",
    )(side, a2, a1, a0, weight)


def chip_sum_kernel(keep_ref, near_ref, o_ref):
    o_ref[...] = (keep_ref[...] + near_ref[...].astype(F32)).astype(BF16)


def chip_sum(keep, near):
    return pl.pallas_call(
        chip_sum_kernel,
        out_shape=jax.ShapeDtypeStruct(keep.shape, BF16),
        in_specs=[VMEM_SPEC] * 2,
        out_specs=VMEM_SPEC,
        name="chip_sum",
    )(keep, near)


def patch_kernel(cols, mine_ref, far_ref, res_ref, o_ref, whole_ref):
    chans = mine_ref.shape[1]
    rows = mine_ref.shape[0] // cols
    block = mine_ref[...].astype(F32) + far_ref[...].astype(F32) + res_ref[...].astype(F32)
    for part in range(chans // 128):
        whole_ref[part] = block[:, part * 128 : (part + 1) * 128]
    for p in range(rows // 2):
        for b in range(2):
            for e in range(2):
                for part in range(chans // 128):
                    lane = (b * 2 + e) * chans + part * 128
                    o_ref[p * cols // 2 : (p + 1) * cols // 2, lane : lane + 128] = whole_ref[
                        part, pl.ds((2 * p + b) * cols + e, cols // 2, stride=2), :
                    ].astype(BF16)


def patch_rows(mine, far, res, cols):
    tokens, chans = mine.shape

    def kernel(*refs):
        patch_kernel(cols, *refs)

    return pl.pallas_call(
        kernel,
        out_shape=jax.ShapeDtypeStruct((tokens // 4, 4 * chans), BF16),
        in_specs=[VMEM_SPEC] * 3,
        out_specs=VMEM_SPEC,
        scratch_shapes=[pltpu.VMEM((chans // 128, tokens, 128), F32)],
        name="patch_rows",
    )(mine, far, res)


def embed_kernel(me_ref, role_ref, mine_ref, near_ref, w0, w1, w2, w3, o_ref):
    half = mine_ref.shape[0]
    depth = w0.shape[1]
    core = me_ref[0] & 1
    for side, ref in ((core, mine_ref), (1 - core, near_ref)):
        total = None
        for k, w_ref in enumerate((w0, w1, w2, w3)):
            lanes = pl.ds(pl.multiple_of((role_ref[0] ^ k) * depth, depth), depth)
            part = dot_nt(ref[:, lanes], w_ref[...])
            total = part if total is None else total + part
        o_ref[pl.ds(pl.multiple_of(side * half, 16), half), :] = total.astype(BF16)


def embed_tokens(me, role, mine, near, weights):
    return pl.pallas_call(
        embed_kernel,
        out_shape=jax.ShapeDtypeStruct((2 * mine.shape[0], weights[0].shape[0]), BF16),
        in_specs=[SMEM_SPEC] * 2 + [VMEM_SPEC] * 6,
        out_specs=VMEM_SPEC,
        name="embed_tokens",
    )(me, role, mine, near, *weights)


def own_column(weight, index):
    return lax.dynamic_index_in_dim(weight.T, index, 0, keepdims=False)


def per_device(latent, conv_first, conv_second, embed_weight, qkv_weight):
    col_count = latent.shape[2]
    chan_count = latent.shape[3]
    lane_count = 4
    me = lax.axis_index("narrow")
    core = me % 2
    chans_here = chan_count // lane_count

    odd = lax.axis_index("wide") % NY == 1
    role = jnp.where(odd, me ^ 2, me)
    me_ref = me.astype(jnp.int32).reshape(1)

    mine = latent.reshape(-1, chan_count)
    far = other(mine, 2)
    near = other(mine, 1)
    cross = other(far, 1)
    old = jnp.stack([delayed(mine, 2), delayed(mine, 1)])
    old_far = other(old, 2)
    old_near = other(old, 1)
    old_cross = other(old_far, 1)

    pick = (
        lax.broadcasted_iota(jnp.int32, (chan_count, chans_here), 0)
        == lane_count * lax.broadcasted_iota(jnp.int32, (chan_count, chans_here), 1) + role
    ).astype(BF16)
    first_shard = own_column(conv_first, role).reshape(-1, 128)
    second_shard = jnp.dot(
        conv_second.T.reshape(-1, chan_count), pick, preferred_element_type=F32
    ).astype(BF16)
    second_shard = second_shard.reshape(lane_count, 3, 9, chans_here)
    second_shard = jnp.moveaxis(second_shard, 1, 2).reshape(-1, 128)
    quarter = embed_weight.shape[0] // 4
    embed_shard = lax.dynamic_slice_in_dim(embed_weight.T, role * quarter, quarter, axis=1)
    embed_shard = embed_shard.reshape(-1, 128)
    shards = jnp.concatenate([first_shard, second_shard, embed_shard])
    by_z = spread(shards, "wide", ALONG_Z)
    split = first_shard.shape[0]
    conv_weights = spread(by_z[:, : 2 * split], BOTH, ALONG_XY)
    conv_weights = in_wide_order(conv_weights, (2 * split, 128))
    first_weight = conv_weights[:, :split].reshape(chans_here, -1)
    second_weight = conv_weights[:, split:].reshape(chan_count, -1)
    embed_mine = spread(by_z[:, 2 * split :], BOTH, ALONG_XY)
    embed_mine = in_wide_order(embed_mine, embed_shard.shape).reshape(-1, quarter)
    embed_far = other(embed_mine, 2)
    embed_near = other(embed_mine, 1)
    embed_cross = other(embed_far, 1)

    activated, residual = first_conv(
        me_ref, (mine, near, far, cross), (old, old_near, old_far, old_cross),
        first_weight, col_count,
    )
    keep, send = second_conv(
        core.astype(jnp.int32).reshape(1),
        delayed(activated, 2),
        delayed(activated, 1),
        activated,
        second_weight,
        col_count,
    )
    summed = chip_sum(keep, other(send, 1))
    patches = patch_rows(summed, other(summed, 2), residual, col_count)
    embedded = embed_tokens(
        me_ref,
        role.astype(jnp.int32).reshape(1),
        patches,
        other(patches, 1),
        (embed_mine, embed_near, embed_far, embed_cross),
    )

    heads_here = qkv_weight.shape[2] // HEAD_DIM
    token_count = embedded.shape[0]
    key_raw = jnp.dot(embedded, qkv_weight[1], preferred_element_type=F32).astype(BF16).astype(F32)
    val_rows = jnp.dot(embedded, qkv_weight[2], preferred_element_type=F32).astype(BF16)
    query_raw = (
        jnp.dot(embedded, qkv_weight[0], preferred_element_type=F32).astype(BF16).astype(F32)
    )
    query_feat = (
        (jax.nn.elu(query_raw) + 1.0).astype(BF16).reshape(token_count, heads_here, HEAD_DIM)
    )
    key_feat = (jax.nn.elu(key_raw) + 1.0).astype(BF16).reshape(token_count, heads_here, HEAD_DIM)
    val_heads = val_rows.reshape(token_count, heads_here, HEAD_DIM)
    scores = jnp.einsum("thd,shd->hts", query_feat, key_feat, preferred_element_type=F32)
    row_ids = lax.broadcasted_iota(jnp.int32, (token_count, token_count), 0)
    col_ids = lax.broadcasted_iota(jnp.int32, (token_count, token_count), 1)
    scores = jnp.where((col_ids <= row_ids)[None], scores, 0.0)
    local_den = jnp.sum(scores, axis=-1)
    local_num = jnp.einsum(
        "hts,she->the", scores.astype(BF16), val_heads, preferred_element_type=F32
    )
    state_local = jnp.einsum("thd,the->hde", key_feat, val_heads, preferred_element_type=F32)
    key_local = jnp.sum(key_feat, axis=0, dtype=F32)
    flat_state = jnp.concatenate([state_local.reshape(-1), key_local.reshape(-1)])
    length_all = flat_state.shape[0]
    peer_count = lax.axis_size("wide")
    per_peer = -(-length_all // peer_count)
    piece_grid = jnp.pad(flat_state, (0, per_peer * peer_count - length_all)).reshape(
        peer_count, per_peer
    )
    lower_ones = (
        lax.broadcasted_iota(jnp.int32, (peer_count, peer_count), 1)
        < lax.broadcasted_iota(jnp.int32, (peer_count, peer_count), 0)
    ).astype(F32)
    arrived = lax.all_to_all(
        piece_grid.astype(BF16), "wide", split_axis=0, concat_axis=0, tiled=True
    )
    partial_sums = jnp.dot(lower_ones, arrived.astype(F32), precision=lax.Precision.HIGHEST)
    spread_back = lax.all_to_all(
        partial_sums.astype(BF16), "wide", split_axis=0, concat_axis=0, tiled=True
    ).astype(F32)
    flat_prefix = spread_back.reshape(-1)[:length_all]
    state_size = state_local.size
    state_prev = flat_prefix[:state_size].reshape(state_local.shape)
    key_prev = flat_prefix[state_size:].reshape(key_local.shape)
    query_wide = query_feat.astype(F32)
    carried_num = jnp.einsum(
        "thd,hde->the", query_wide, state_prev, precision=lax.Precision.HIGHEST
    )
    carried_den = jnp.einsum("thd,hd->th", query_wide, key_prev, precision=lax.Precision.HIGHEST)
    result = (local_num + carried_num) / (local_den.T + carried_den)[..., None]
    return result.astype(BF16).reshape(token_count, heads_here * HEAD_DIM)


def solution(mesh):
    return jax.shard_map(
        per_device,
        mesh=mesh,
        in_specs=(
            P("wide", "narrow", None, None),
            P(None, "wide"),
            P(None, "wide"),
            P(None, "wide"),
            P(None, None, "narrow"),
        ),
        out_specs=P("wide", "narrow"),
        check_vma=False,
    )
```

```python
import jax
import jax.numpy as jnp
from jax import lax
from jax.experimental import pallas as pl
from jax.experimental.pallas import tpu as pltpu
from jax.sharding import PartitionSpec as P


HEAD_DIM = 112
NX, NZ, NY = 4, 8, 2
BOTH = ("wide", "narrow")
BF16 = jnp.bfloat16
F32 = jnp.float32


def wide_index(x, z, y):
    return (x * NZ + z) * NY + y


ALONG_Z = [
    [wide_index(x, z, y) for z in range(NZ)] for x in range(NX) for y in range(NY)
]
ALONG_XY = [
    [wide_index(x, z, y) * 4 + (role ^ 2 * y) for x in range(NX) for y in range(NY)]
    for z in range(NZ)
    for role in range(4)
]


def delayed(x, by):
    size = lax.axis_size("wide")
    pairs = [
        (4 * i + n, 4 * (i + by) + (n ^ 2 * (by % 2))) for i in range(size - by) for n in range(4)
    ]
    return lax.ppermute(x, BOTH, pairs)


def other(x, mask):
    return lax.ppermute(x, "narrow", [(i, i ^ mask) for i in range(4)])


def spread(x, axis, groups):
    count = len(groups[0])
    copies = jnp.broadcast_to(x[None], (count,) + x.shape)
    return lax.all_to_all(copies, axis, 0, 0, axis_index_groups=groups, tiled=True)


def in_wide_order(by_xy, shape):
    blocks = by_xy.reshape((NX, NY, NZ) + shape)
    return jnp.moveaxis(blocks, 1, 2).reshape((NX * NY * NZ,) + shape)


def dot_nt(a, b):
    return lax.dot_general(a, b, (((1,), (1,)), ((), ())), preferred_element_type=F32)


def column_sum(prod_ref, rows, cols, width):
    col = lax.broadcasted_iota(jnp.int32, (rows, 1), 0) % cols
    left = prod_ref[7 : 7 + rows, :width]
    mid = prod_ref[8 : 8 + rows, width : 2 * width]
    right = prod_ref[9 : 9 + rows, 2 * width : 3 * width]
    return jnp.where(col != 0, left, 0.0) + mid + jnp.where(col != cols - 1, right, 0.0)


def first_conv_kernel(
    cols, me_ref, now0, now1, now2, now3, old0, old1, old2, old3, w_ref, o_ref, res_ref,
    pad_ref, tap_ref, prod_ref,
):
    strip = now0.shape[0]
    tokens = 4 * strip
    width = w_ref.shape[0]
    me = me_ref[0]
    pad_ref[:, :cols, :] = jnp.zeros((3, cols, 256), BF16)
    pad_ref[:, cols + tokens :, :] = jnp.zeros((3, cols, 256), BF16)
    for k, (now, old) in enumerate(((now0, old0), (now1, old1), (now2, old2), (now3, old3))):
        place = pl.ds(pl.multiple_of(cols + (me ^ k) * strip, 16), strip)
        pad_ref[2, place, :] = now[...]
        pad_ref[0, place, :] = old[0]
        place = pl.ds(pl.multiple_of(cols + (me ^ k ^ 2) * strip, 16), strip)
        pad_ref[1, place, :] = old[1]
    half = tokens // 2
    res_ref[...] = pad_ref[2, pl.ds(pl.multiple_of(cols + (me & 1) * half, 16), half), :]
    for tap in range(27):
        tap_ref[tap // 3, tap % 3 * width : (tap % 3 + 1) * width, :] = w_ref[
            :, tap * 256 : (tap + 1) * 256
        ]
    prod_ref[0:8, :] = jnp.zeros((8, 3 * width), F32)
    prod_ref[8 + tokens :, :] = jnp.zeros((8, 3 * width), F32)
    chunk = tokens // 4
    for part in range(4):
        total = jnp.zeros((chunk, 3 * width), F32)
        for tap in range(9):
            start = part * chunk + tap % 3 * cols
            total += dot_nt(pad_ref[tap // 3, start : start + chunk, :], tap_ref[tap])
        prod_ref[8 + part * chunk : 8 + (part + 1) * chunk, :] = total
    first = column_sum(prod_ref, tokens, cols, width)
    o_ref[...] = (first / (1.0 + jnp.exp(-first))).astype(BF16)


VMEM_SPEC = pl.BlockSpec(memory_space=pltpu.VMEM)
SMEM_SPEC = pl.BlockSpec(memory_space=pltpu.SMEM)


def first_conv(me, now, old, weight, cols):
    tokens = 4 * now[0].shape[0]
    width = weight.shape[0]

    def kernel(*refs):
        first_conv_kernel(cols, *refs)

    return pl.pallas_call(
        kernel,
        out_shape=(
            jax.ShapeDtypeStruct((tokens, width), BF16),
            jax.ShapeDtypeStruct((tokens // 2, 256), BF16),
        ),
        in_specs=[SMEM_SPEC] + [VMEM_SPEC] * 9,
        out_specs=(VMEM_SPEC, VMEM_SPEC),
        scratch_shapes=[
            pltpu.VMEM((3, tokens + 2 * cols, 256), BF16),
            pltpu.VMEM((9, 3 * width, 256), BF16),
            pltpu.VMEM((tokens + 16, 3 * width), F32),
        ],
        name="first_conv",
    )(me, *now, *old, weight)


def second_conv_kernel(
    cols, side_ref, a2_ref, a1_ref, a0_ref, w_ref, keep_ref, send_ref, pad_ref, tap_ref, prod_ref
):
    tokens, chans = a0_ref.shape
    depth = 3 * chans
    width = w_ref.shape[0]
    half = tokens // 2
    pad_ref[:cols, :] = jnp.zeros((cols, depth), BF16)
    pad_ref[cols + tokens :, :] = jnp.zeros((cols, depth), BF16)
    pad_ref[cols : cols + tokens, :] = jnp.concatenate(
        [a2_ref[...], a1_ref[...], a0_ref[...]], axis=1
    )
    for tap in range(9):
        tap_ref[tap // 3, tap % 3 * width : (tap % 3 + 1) * width, :] = w_ref[
            :, tap * depth : (tap + 1) * depth
        ]
    prod_ref[0:8, :] = jnp.zeros((8, 3 * width), F32)
    prod_ref[8 + tokens :, :] = jnp.zeros((8, 3 * width), F32)
    chunk = tokens // 4
    for part in range(4):
        total = jnp.zeros((chunk, 3 * width), F32)
        for tap in range(3):
            start = part * chunk + tap * cols
            total += dot_nt(pad_ref[start : start + chunk, :], tap_ref[tap])
        prod_ref[8 + part * chunk : 8 + (part + 1) * chunk, :] = total
    summed = column_sum(prod_ref, tokens, cols, width)

    @pl.when(side_ref[0] == 0)
    def _():
        keep_ref[...] = summed[:half]
        send_ref[...] = summed[half:].astype(BF16)

    @pl.when(side_ref[0] == 1)
    def _():
        keep_ref[...] = summed[half:]
        send_ref[...] = summed[:half].astype(BF16)


def second_conv(side, a2, a1, a0, weight, cols):
    tokens, chans = a0.shape
    width = weight.shape[0]

    def kernel(*refs):
        second_conv_kernel(cols, *refs)

    return pl.pallas_call(
        kernel,
        out_shape=(
            jax.ShapeDtypeStruct((tokens // 2, width), F32),
            jax.ShapeDtypeStruct((tokens // 2, width), BF16),
        ),
        in_specs=[SMEM_SPEC] + [VMEM_SPEC] * 4,
        out_specs=(VMEM_SPEC, VMEM_SPEC),
        scratch_shapes=[
            pltpu.VMEM((tokens + 2 * cols, 3 * chans), BF16),
            pltpu.VMEM((3, 3 * width, 3 * chans), BF16),
            pltpu.VMEM((tokens + 16, 3 * width), F32),
        ],
        name="second_conv",
    )(side, a2, a1, a0, weight)


def chip_sum_kernel(keep_ref, near_ref, o_ref):
    o_ref[...] = (keep_ref[...] + near_ref[...].astype(F32)).astype(BF16)


def chip_sum(keep, near):
    return pl.pallas_call(
        chip_sum_kernel,
        out_shape=jax.ShapeDtypeStruct(keep.shape, BF16),
        in_specs=[VMEM_SPEC] * 2,
        out_specs=VMEM_SPEC,
        name="chip_sum",
    )(keep, near)


def patch_kernel(cols, mine_ref, far_ref, res_ref, o_ref, whole_ref):
    chans = mine_ref.shape[1]
    rows = mine_ref.shape[0] // cols
    block = mine_ref[...].astype(F32) + far_ref[...].astype(F32) + res_ref[...].astype(F32)
    for part in range(chans // 128):
        whole_ref[part] = block[:, part * 128 : (part + 1) * 128]
    for p in range(rows // 2):
        for b in range(2):
            for e in range(2):
                for part in range(chans // 128):
                    lane = (b * 2 + e) * chans + part * 128
                    o_ref[p * cols // 2 : (p + 1) * cols // 2, lane : lane + 128] = whole_ref[
                        part, pl.ds((2 * p + b) * cols + e, cols // 2, stride=2), :
                    ].astype(BF16)


def patch_rows(mine, far, res, cols):
    tokens, chans = mine.shape

    def kernel(*refs):
        patch_kernel(cols, *refs)

    return pl.pallas_call(
        kernel,
        out_shape=jax.ShapeDtypeStruct((tokens // 4, 4 * chans), BF16),
        in_specs=[VMEM_SPEC] * 3,
        out_specs=VMEM_SPEC,
        scratch_shapes=[pltpu.VMEM((chans // 128, tokens, 128), F32)],
        name="patch_rows",
    )(mine, far, res)


def embed_kernel(me_ref, role_ref, mine_ref, near_ref, w0, w1, w2, w3, o_ref, all_ref):
    half = mine_ref.shape[0]
    width, depth = w0.shape
    core = me_ref[0] & 1
    for side, ref in ((core, mine_ref), (1 - core, near_ref)):
        all_ref[pl.ds(pl.multiple_of(side * half, 16), half), :] = ref[...]
    for start in range(0, width, 256):
        end = min(start + 256, width)
        total = None
        for k, w_ref in enumerate((w0, w1, w2, w3)):
            lanes = pl.ds(pl.multiple_of((role_ref[0] ^ k) * depth, depth), depth)
            part = dot_nt(all_ref[:, lanes], w_ref[start:end, :])
            total = part if total is None else total + part
        o_ref[:, start:end] = total.astype(BF16)


def embed_tokens(me, role, mine, near, weights):
    tokens = 2 * mine.shape[0]
    return pl.pallas_call(
        embed_kernel,
        out_shape=jax.ShapeDtypeStruct((tokens, weights[0].shape[0]), BF16),
        in_specs=[SMEM_SPEC] * 2 + [VMEM_SPEC] * 6,
        out_specs=VMEM_SPEC,
        scratch_shapes=[pltpu.VMEM((tokens, mine.shape[1]), BF16)],
        name="embed_tokens",
    )(me, role, mine, near, *weights)


def own_column(weight, index):
    return lax.dynamic_index_in_dim(weight.T, index, 0, keepdims=False)


def per_device(latent, conv_first, conv_second, embed_weight, qkv_weight):
    col_count = latent.shape[2]
    chan_count = latent.shape[3]
    lane_count = 4
    me = lax.axis_index("narrow")
    core = me % 2
    chans_here = chan_count // lane_count

    odd = lax.axis_index("wide") % NY == 1
    role = jnp.where(odd, me ^ 2, me)
    me_ref = me.astype(jnp.int32).reshape(1)

    mine = latent.reshape(-1, chan_count)
    far = other(mine, 2)
    near = other(mine, 1)
    cross = other(far, 1)
    old = jnp.stack([delayed(mine, 2), delayed(mine, 1)])
    old_far = other(old, 2)
    old_near = other(old, 1)
    old_cross = other(old_far, 1)

    pick = (
        lax.broadcasted_iota(jnp.int32, (chan_count, chans_here), 0)
        == lane_count * lax.broadcasted_iota(jnp.int32, (chan_count, chans_here), 1) + role
    ).astype(BF16)
    first_shard = own_column(conv_first, role).reshape(-1, 128)
    second_shard = jnp.dot(
        conv_second.T.reshape(-1, chan_count), pick, preferred_element_type=F32
    ).astype(BF16)
    second_shard = second_shard.reshape(lane_count, 3, 9, chans_here)
    second_shard = jnp.moveaxis(second_shard, 1, 2).reshape(-1, 128)
    quarter = embed_weight.shape[0] // 4
    embed_shard = lax.dynamic_slice_in_dim(embed_weight.T, role * quarter, quarter, axis=1)
    embed_shard = embed_shard.reshape(-1, 128)
    shards = jnp.concatenate([first_shard, second_shard, embed_shard])
    by_z = spread(shards, "wide", ALONG_Z)
    split = first_shard.shape[0]
    conv_weights = spread(by_z[:, : 2 * split], BOTH, ALONG_XY)
    conv_weights = in_wide_order(conv_weights, (2 * split, 128))
    first_weight = conv_weights[:, :split].reshape(chans_here, -1)
    second_weight = conv_weights[:, split:].reshape(chan_count, -1)
    embed_mine = spread(by_z[:, 2 * split :], BOTH, ALONG_XY)
    embed_mine = in_wide_order(embed_mine, embed_shard.shape).reshape(-1, quarter)
    embed_far = other(embed_mine, 2)
    embed_near = other(embed_mine, 1)
    embed_cross = other(embed_far, 1)

    activated, residual = first_conv(
        me_ref, (mine, near, far, cross), (old, old_near, old_far, old_cross),
        first_weight, col_count,
    )
    keep, send = second_conv(
        core.astype(jnp.int32).reshape(1),
        delayed(activated, 2),
        delayed(activated, 1),
        activated,
        second_weight,
        col_count,
    )
    summed = chip_sum(keep, other(send, 1))
    patches = patch_rows(summed, other(summed, 2), residual, col_count)
    embedded = embed_tokens(
        me_ref,
        role.astype(jnp.int32).reshape(1),
        patches,
        other(patches, 1),
        (embed_mine, embed_near, embed_far, embed_cross),
    )

    heads_here = qkv_weight.shape[2] // HEAD_DIM
    token_count = embedded.shape[0]
    key_raw = jnp.dot(embedded, qkv_weight[1], preferred_element_type=F32).astype(BF16).astype(F32)
    val_rows = jnp.dot(embedded, qkv_weight[2], preferred_element_type=F32).astype(BF16)
    query_raw = (
        jnp.dot(embedded, qkv_weight[0], preferred_element_type=F32).astype(BF16).astype(F32)
    )
    query_feat = (
        (jax.nn.elu(query_raw) + 1.0).astype(BF16).reshape(token_count, heads_here, HEAD_DIM)
    )
    key_feat = (jax.nn.elu(key_raw) + 1.0).astype(BF16).reshape(token_count, heads_here, HEAD_DIM)
    val_heads = val_rows.reshape(token_count, heads_here, HEAD_DIM)
    scores = jnp.einsum("thd,shd->hts", query_feat, key_feat, preferred_element_type=F32)
    row_ids = lax.broadcasted_iota(jnp.int32, (token_count, token_count), 0)
    col_ids = lax.broadcasted_iota(jnp.int32, (token_count, token_count), 1)
    scores = jnp.where((col_ids <= row_ids)[None], scores, 0.0)
    local_den = jnp.sum(scores, axis=-1)
    local_num = jnp.einsum(
        "hts,she->the", scores.astype(BF16), val_heads, preferred_element_type=F32
    )
    state_local = jnp.einsum("thd,the->hde", key_feat, val_heads, preferred_element_type=F32)
    key_local = jnp.sum(key_feat, axis=0, dtype=F32)
    flat_state = jnp.concatenate([state_local.reshape(-1), key_local.reshape(-1)])
    length_all = flat_state.shape[0]
    peer_count = lax.axis_size("wide")
    per_peer = -(-length_all // peer_count)
    piece_grid = jnp.pad(flat_state, (0, per_peer * peer_count - length_all)).reshape(
        peer_count, per_peer
    )
    lower_ones = (
        lax.broadcasted_iota(jnp.int32, (peer_count, peer_count), 1)
        < lax.broadcasted_iota(jnp.int32, (peer_count, peer_count), 0)
    ).astype(F32)
    arrived = lax.all_to_all(
        piece_grid.astype(BF16), "wide", split_axis=0, concat_axis=0, tiled=True
    )
    partial_sums = jnp.dot(lower_ones, arrived.astype(F32), precision=lax.Precision.HIGHEST)
    spread_back = lax.all_to_all(
        partial_sums.astype(BF16), "wide", split_axis=0, concat_axis=0, tiled=True
    ).astype(F32)
    flat_prefix = spread_back.reshape(-1)[:length_all]
    state_size = state_local.size
    state_prev = flat_prefix[:state_size].reshape(state_local.shape)
    key_prev = flat_prefix[state_size:].reshape(key_local.shape)
    query_wide = query_feat.astype(F32)
    carried_num = jnp.einsum(
        "thd,hde->the", query_wide, state_prev, precision=lax.Precision.HIGHEST
    )
    carried_den = jnp.einsum("thd,hd->th", query_wide, key_prev, precision=lax.Precision.HIGHEST)
    result = (local_num + carried_num) / (local_den.T + carried_den)[..., None]
    return result.astype(BF16).reshape(token_count, heads_here * HEAD_DIM)


def solution(mesh):
    return jax.shard_map(
        per_device,
        mesh=mesh,
        in_specs=(
            P("wide", "narrow", None, None),
            P(None, "wide"),
            P(None, "wide"),
            P(None, "wide"),
            P(None, None, "narrow"),
        ),
        out_specs=P("wide", "narrow"),
        check_vma=False,
    )
```

```python
import jax
import jax.numpy as jnp
from jax import lax
from jax.experimental import pallas as pl
from jax.experimental.pallas import tpu as pltpu
from jax.sharding import PartitionSpec as P


HEAD_DIM = 112
NX, NZ, NY = 4, 8, 2
BOTH = ("wide", "narrow")
BF16 = jnp.bfloat16
F32 = jnp.float32


def wide_index(x, z, y):
    return (x * NZ + z) * NY + y


ALONG_Z = [
    [wide_index(x, z, y) for z in range(NZ)] for x in range(NX) for y in range(NY)
]
ALONG_XY = [
    [wide_index(x, z, y) * 4 + (role ^ 2 * y) for x in range(NX) for y in range(NY)]
    for z in range(NZ)
    for role in range(4)
]


def delayed(x, by):
    size = lax.axis_size("wide")
    pairs = [
        (4 * i + n, 4 * (i + by) + (n ^ 2 * (by % 2))) for i in range(size - by) for n in range(4)
    ]
    return lax.ppermute(x, BOTH, pairs)


def other(x, mask):
    return lax.ppermute(x, "narrow", [(i, i ^ mask) for i in range(4)])


def spread(x, axis, groups):
    count = len(groups[0])
    copies = jnp.broadcast_to(x[None], (count,) + x.shape)
    return lax.all_to_all(copies, axis, 0, 0, axis_index_groups=groups, tiled=True)


def in_wide_order(by_xy, shape):
    blocks = by_xy.reshape((NX, NY, NZ) + shape)
    return jnp.moveaxis(blocks, 1, 2).reshape((NX * NY * NZ,) + shape)


def dot_nt(a, b):
    return lax.dot_general(a, b, (((1,), (1,)), ((), ())), preferred_element_type=F32)


def column_sum(prod_ref, rows, cols, width):
    col = lax.broadcasted_iota(jnp.int32, (rows, 1), 0) % cols
    left = prod_ref[7 : 7 + rows, :width]
    mid = prod_ref[8 : 8 + rows, width : 2 * width]
    right = prod_ref[9 : 9 + rows, 2 * width : 3 * width]
    return jnp.where(col != 0, left, 0.0) + mid + jnp.where(col != cols - 1, right, 0.0)


def first_conv_kernel(
    cols, me_ref, now0, now1, now2, now3, old0, old1, old2, old3, w_ref, o_ref, res_ref,
    pad_ref, tap_ref, prod_ref,
):
    strip = now0.shape[0]
    tokens = 4 * strip
    width = w_ref.shape[0]
    me = me_ref[0]
    pad_ref[:, :cols, :] = jnp.zeros((3, cols, 256), BF16)
    pad_ref[:, cols + tokens :, :] = jnp.zeros((3, cols, 256), BF16)
    for k, (now, old) in enumerate(((now0, old0), (now1, old1), (now2, old2), (now3, old3))):
        place = pl.ds(pl.multiple_of(cols + (me ^ k) * strip, 16), strip)
        pad_ref[2, place, :] = now[...]
        pad_ref[0, place, :] = old[0]
        place = pl.ds(pl.multiple_of(cols + (me ^ k ^ 2) * strip, 16), strip)
        pad_ref[1, place, :] = old[1]
    half = tokens // 2
    res_ref[...] = pad_ref[2, pl.ds(pl.multiple_of(cols + (me & 1) * half, 16), half), :]
    for tap in range(27):
        tap_ref[tap // 3, tap % 3 * width : (tap % 3 + 1) * width, :] = w_ref[
            :, tap * 256 : (tap + 1) * 256
        ]
    prod_ref[0:8, :] = jnp.zeros((8, 3 * width), F32)
    prod_ref[8 + tokens :, :] = jnp.zeros((8, 3 * width), F32)
    chunk = tokens // 4
    for part in range(4):
        total = jnp.zeros((chunk, 3 * width), F32)
        for tap in range(9):
            start = part * chunk + tap % 3 * cols
            total += dot_nt(pad_ref[tap // 3, start : start + chunk, :], tap_ref[tap])
        prod_ref[8 + part * chunk : 8 + (part + 1) * chunk, :] = total
    first = column_sum(prod_ref, tokens, cols, width)
    o_ref[...] = (first / (1.0 + jnp.exp(-first))).astype(BF16)


VMEM_SPEC = pl.BlockSpec(memory_space=pltpu.VMEM)
SMEM_SPEC = pl.BlockSpec(memory_space=pltpu.SMEM)


def first_conv(me, now, old, weight, cols):
    tokens = 4 * now[0].shape[0]
    width = weight.shape[0]

    def kernel(*refs):
        first_conv_kernel(cols, *refs)

    return pl.pallas_call(
        kernel,
        out_shape=(
            jax.ShapeDtypeStruct((tokens, width), BF16),
            jax.ShapeDtypeStruct((tokens // 2, 256), BF16),
        ),
        in_specs=[SMEM_SPEC] + [VMEM_SPEC] * 9,
        out_specs=(VMEM_SPEC, VMEM_SPEC),
        scratch_shapes=[
            pltpu.VMEM((3, tokens + 2 * cols, 256), BF16),
            pltpu.VMEM((9, 3 * width, 256), BF16),
            pltpu.VMEM((tokens + 16, 3 * width), F32),
        ],
        name="first_conv",
    )(me, *now, *old, weight)


def second_conv_kernel(
    cols, side_ref, a2_ref, a1_ref, a0_ref, w_ref, keep_ref, send_ref, pad_ref, tap_ref, prod_ref
):
    tokens, chans = a0_ref.shape
    depth = 3 * chans
    width = w_ref.shape[0]
    half = tokens // 2
    pad_ref[:cols, :] = jnp.zeros((cols, depth), BF16)
    pad_ref[cols + tokens :, :] = jnp.zeros((cols, depth), BF16)
    pad_ref[cols : cols + tokens, :] = jnp.concatenate(
        [a2_ref[...], a1_ref[...], a0_ref[...]], axis=1
    )
    for tap in range(9):
        tap_ref[tap // 3, tap % 3 * width : (tap % 3 + 1) * width, :] = w_ref[
            :, tap * depth : (tap + 1) * depth
        ]
    prod_ref[0:8, :] = jnp.zeros((8, 3 * width), F32)
    prod_ref[8 + tokens :, :] = jnp.zeros((8, 3 * width), F32)
    chunk = tokens // 4
    for part in range(4):
        total = jnp.zeros((chunk, 3 * width), F32)
        for tap in range(3):
            start = part * chunk + tap * cols
            total += dot_nt(pad_ref[start : start + chunk, :], tap_ref[tap])
        prod_ref[8 + part * chunk : 8 + (part + 1) * chunk, :] = total
    summed = column_sum(prod_ref, tokens, cols, width)

    @pl.when(side_ref[0] == 0)
    def _():
        keep_ref[...] = summed[:half]
        send_ref[...] = summed[half:].astype(BF16)

    @pl.when(side_ref[0] == 1)
    def _():
        keep_ref[...] = summed[half:]
        send_ref[...] = summed[:half].astype(BF16)


def second_conv(side, a2, a1, a0, weight, cols):
    tokens, chans = a0.shape
    width = weight.shape[0]

    def kernel(*refs):
        second_conv_kernel(cols, *refs)

    return pl.pallas_call(
        kernel,
        out_shape=(
            jax.ShapeDtypeStruct((tokens // 2, width), F32),
            jax.ShapeDtypeStruct((tokens // 2, width), BF16),
        ),
        in_specs=[SMEM_SPEC] + [VMEM_SPEC] * 4,
        out_specs=(VMEM_SPEC, VMEM_SPEC),
        scratch_shapes=[
            pltpu.VMEM((tokens + 2 * cols, 3 * chans), BF16),
            pltpu.VMEM((3, 3 * width, 3 * chans), BF16),
            pltpu.VMEM((tokens + 16, 3 * width), F32),
        ],
        name="second_conv",
    )(side, a2, a1, a0, weight)


def chip_sum_kernel(keep_ref, near_ref, o_ref):
    o_ref[...] = (keep_ref[...] + near_ref[...].astype(F32)).astype(BF16)


def chip_sum(keep, near):
    return pl.pallas_call(
        chip_sum_kernel,
        out_shape=jax.ShapeDtypeStruct(keep.shape, BF16),
        in_specs=[VMEM_SPEC] * 2,
        out_specs=VMEM_SPEC,
        name="chip_sum",
    )(keep, near)


def patch_kernel(cols, mine_ref, far_ref, res_ref, o_ref, whole_ref):
    chans = mine_ref.shape[1]
    rows = mine_ref.shape[0] // cols
    block = mine_ref[...].astype(F32) + far_ref[...].astype(F32) + res_ref[...].astype(F32)
    for part in range(chans // 128):
        whole_ref[part] = block[:, part * 128 : (part + 1) * 128]
    for p in range(rows // 2):
        for b in range(2):
            for e in range(2):
                for part in range(chans // 128):
                    lane = (b * 2 + e) * chans + part * 128
                    o_ref[p * cols // 2 : (p + 1) * cols // 2, lane : lane + 128] = whole_ref[
                        part, pl.ds((2 * p + b) * cols + e, cols // 2, stride=2), :
                    ].astype(BF16)


def patch_rows(mine, far, res, cols):
    tokens, chans = mine.shape

    def kernel(*refs):
        patch_kernel(cols, *refs)

    return pl.pallas_call(
        kernel,
        out_shape=jax.ShapeDtypeStruct((tokens // 4, 4 * chans), BF16),
        in_specs=[VMEM_SPEC] * 3,
        out_specs=VMEM_SPEC,
        scratch_shapes=[pltpu.VMEM((chans // 128, tokens, 128), F32)],
        name="patch_rows",
    )(mine, far, res)


def embed_kernel(me_ref, role_ref, mine_ref, near_ref, w0, w1, w2, w3, o_ref, all_ref):
    half = mine_ref.shape[0]
    width, depth = w0.shape
    core = me_ref[0] & 1
    for side, ref in ((core, mine_ref), (1 - core, near_ref)):
        all_ref[pl.ds(pl.multiple_of(side * half, 16), half), :] = ref[...]
    for start in range(0, width, 256):
        end = min(start + 256, width)
        total = None
        for k, w_ref in enumerate((w0, w1, w2, w3)):
            lanes = pl.ds(pl.multiple_of((role_ref[0] ^ k) * depth, depth), depth)
            part = dot_nt(all_ref[:, lanes], w_ref[start:end, :])
            total = part if total is None else total + part
        o_ref[:, start:end] = total.astype(BF16)


def embed_tokens(me, role, mine, near, weights):
    tokens = 2 * mine.shape[0]
    return pl.pallas_call(
        embed_kernel,
        out_shape=jax.ShapeDtypeStruct((tokens, weights[0].shape[0]), BF16),
        in_specs=[SMEM_SPEC] * 2 + [VMEM_SPEC] * 6,
        out_specs=VMEM_SPEC,
        scratch_shapes=[pltpu.VMEM((tokens, mine.shape[1]), BF16)],
        name="embed_tokens",
    )(me, role, mine, near, *weights)


def own_column(weight, index):
    return lax.dynamic_index_in_dim(weight.T, index, 0, keepdims=False)


def per_device(latent, conv_first, conv_second, embed_weight, qkv_weight):
    col_count = latent.shape[2]
    chan_count = latent.shape[3]
    lane_count = 4
    me = lax.axis_index("narrow")
    core = me % 2
    chans_here = chan_count // lane_count

    odd = lax.axis_index("wide") % NY == 1
    role = jnp.where(odd, me ^ 2, me)
    me_ref = me.astype(jnp.int32).reshape(1)

    mine = latent.reshape(-1, chan_count)
    far = other(mine, 2)
    near = other(mine, 1)
    cross = other(far, 1)
    old = jnp.stack([delayed(mine, 2), delayed(mine, 1)])
    old_far = other(old, 2)
    old_near = other(old, 1)
    old_cross = other(old_far, 1)

    pick = (
        lax.broadcasted_iota(jnp.int32, (chan_count, chans_here), 0)
        == lane_count * lax.broadcasted_iota(jnp.int32, (chan_count, chans_here), 1) + role
    ).astype(BF16)
    first_shard = own_column(conv_first, role).reshape(-1, 128)
    second_shard = jnp.dot(
        conv_second.T.reshape(-1, chan_count), pick, preferred_element_type=F32
    ).astype(BF16)
    second_shard = second_shard.reshape(lane_count, 3, 9, chans_here)
    second_shard = jnp.moveaxis(second_shard, 1, 2).reshape(-1, 128)
    quarter = embed_weight.shape[0] // 4
    embed_shard = lax.dynamic_slice_in_dim(embed_weight.T, role * quarter, quarter, axis=1)
    embed_shard = embed_shard.reshape(-1, 128)
    shards = jnp.concatenate([first_shard, second_shard, embed_shard])
    by_z = spread(shards, "wide", ALONG_Z)
    split = first_shard.shape[0]
    conv_weights = spread(by_z[:, : 2 * split], BOTH, ALONG_XY)
    conv_weights = in_wide_order(conv_weights, (2 * split, 128))
    first_weight = conv_weights[:, :split].reshape(chans_here, -1)
    second_weight = conv_weights[:, split:].reshape(chan_count, -1)
    embed_mine = spread(by_z[:, 2 * split :], BOTH, ALONG_XY)
    embed_mine = in_wide_order(embed_mine, embed_shard.shape).reshape(-1, quarter)
    embed_far = other(embed_mine, 2)
    embed_near = other(embed_mine, 1)
    embed_cross = other(embed_far, 1)

    activated, residual = first_conv(
        me_ref, (mine, near, far, cross), (old, old_near, old_far, old_cross),
        first_weight, col_count,
    )
    keep, send = second_conv(
        core.astype(jnp.int32).reshape(1),
        delayed(activated, 2),
        delayed(activated, 1),
        activated,
        second_weight,
        col_count,
    )
    summed = chip_sum(keep, other(send, 1))
    patches = patch_rows(summed, other(summed, 2), residual, col_count)
    embedded = embed_tokens(
        me_ref,
        role.astype(jnp.int32).reshape(1),
        patches,
        other(patches, 1),
        (embed_mine, embed_near, embed_far, embed_cross),
    )

    heads_here = qkv_weight.shape[2] // HEAD_DIM
    token_count = embedded.shape[0]
    key_raw = jnp.dot(embedded, qkv_weight[1], preferred_element_type=F32).astype(BF16).astype(F32)
    val_rows = jnp.dot(embedded, qkv_weight[2], preferred_element_type=F32).astype(BF16)
    query_raw = (
        jnp.dot(embedded, qkv_weight[0], preferred_element_type=F32).astype(BF16).astype(F32)
    )
    query_feat = (
        (jax.nn.elu(query_raw) + 1.0).astype(BF16).reshape(token_count, heads_here, HEAD_DIM)
    )
    key_feat = (jax.nn.elu(key_raw) + 1.0).astype(BF16).reshape(token_count, heads_here, HEAD_DIM)
    val_heads = val_rows.reshape(token_count, heads_here, HEAD_DIM)
    scores = jnp.einsum("thd,shd->hts", query_feat, key_feat, preferred_element_type=F32)
    row_ids = lax.broadcasted_iota(jnp.int32, (token_count, token_count), 0)
    col_ids = lax.broadcasted_iota(jnp.int32, (token_count, token_count), 1)
    scores = jnp.where((col_ids <= row_ids)[None], scores, 0.0)
    local_den = jnp.sum(scores, axis=-1)
    local_num = jnp.einsum(
        "hts,she->the", scores.astype(BF16), val_heads, preferred_element_type=F32
    )
    state_local = jnp.einsum("thd,the->hde", key_feat, val_heads, preferred_element_type=F32)
    key_local = jnp.sum(key_feat, axis=0, dtype=F32)
    flat_state = jnp.concatenate([state_local.reshape(-1), key_local.reshape(-1)])
    length_all = flat_state.shape[0]
    peer_count = lax.axis_size("wide")
    per_peer = -(-length_all // peer_count)
    piece_grid = jnp.pad(flat_state, (0, per_peer * peer_count - length_all)).reshape(
        peer_count, per_peer
    )
    lower_ones = (
        lax.broadcasted_iota(jnp.int32, (peer_count, peer_count), 1)
        < lax.broadcasted_iota(jnp.int32, (peer_count, peer_count), 0)
    ).astype(BF16)
    arrived = lax.all_to_all(
        piece_grid.astype(BF16), "wide", split_axis=0, concat_axis=0, tiled=True
    )
    partial_sums = jnp.dot(lower_ones, arrived, preferred_element_type=F32)
    spread_back = lax.all_to_all(
        partial_sums.astype(BF16), "wide", split_axis=0, concat_axis=0, tiled=True
    )
    flat_prefix = spread_back.reshape(-1)[:length_all]
    state_size = state_local.size
    state_prev = flat_prefix[:state_size].reshape(state_local.shape)
    key_prev = flat_prefix[state_size:].reshape(key_local.shape)
    carried_num = jnp.einsum(
        "thd,hde->the", query_feat, state_prev, preferred_element_type=F32
    )
    carried_den = jnp.einsum("thd,hd->th", query_feat, key_prev, preferred_element_type=F32)
    result = (local_num + carried_num) / (local_den.T + carried_den)[..., None]
    return result.astype(BF16).reshape(token_count, heads_here * HEAD_DIM)


def solution(mesh):
    return jax.shard_map(
        per_device,
        mesh=mesh,
        in_specs=(
            P("wide", "narrow", None, None),
            P(None, "wide"),
            P(None, "wide"),
            P(None, "wide"),
            P(None, None, "narrow"),
        ),
        out_specs=P("wide", "narrow"),
        check_vma=False,
    )
```

```python
import jax
import jax.numpy as jnp
from jax import lax
from jax.experimental import pallas as pl
from jax.experimental.pallas import tpu as pltpu
from jax.sharding import PartitionSpec as P


HEAD_DIM = 112
NX, NZ, NY = 4, 8, 2
BOTH = ("wide", "narrow")
BF16 = jnp.bfloat16
F32 = jnp.float32


def wide_index(x, z, y):
    return (x * NZ + z) * NY + y


ALONG_Z = [
    [wide_index(x, z, y) for z in range(NZ)] for x in range(NX) for y in range(NY)
]
ALONG_XY = [
    [wide_index(x, z, y) * 4 + (role ^ 2 * y) for x in range(NX) for y in range(NY)]
    for z in range(NZ)
    for role in range(4)
]


def delayed(x, by):
    size = lax.axis_size("wide")
    pairs = [
        (4 * i + n, 4 * (i + by) + (n ^ 2 * (by % 2))) for i in range(size - by) for n in range(4)
    ]
    return lax.ppermute(x, BOTH, pairs)


def other(x, mask):
    return lax.ppermute(x, "narrow", [(i, i ^ mask) for i in range(4)])


def spread(x, axis, groups):
    count = len(groups[0])
    copies = jnp.broadcast_to(x[None], (count,) + x.shape)
    return lax.all_to_all(copies, axis, 0, 0, axis_index_groups=groups, tiled=True)


def in_wide_order(by_xy, shape):
    blocks = by_xy.reshape((NX, NY, NZ) + shape)
    return jnp.moveaxis(blocks, 1, 2).reshape((NX * NY * NZ,) + shape)


def dot_nt(a, b):
    return lax.dot_general(a, b, (((1,), (1,)), ((), ())), preferred_element_type=F32)


def column_sum(prod_ref, rows, cols, width):
    col = lax.broadcasted_iota(jnp.int32, (rows, 1), 0) % cols
    left = prod_ref[7 : 7 + rows, :width]
    mid = prod_ref[8 : 8 + rows, width : 2 * width]
    right = prod_ref[9 : 9 + rows, 2 * width : 3 * width]
    return jnp.where(col != 0, left, 0.0) + mid + jnp.where(col != cols - 1, right, 0.0)


def first_conv_kernel(
    cols, me_ref, now0, now1, now2, now3, old0, old1, old2, old3, w_ref, o_ref, res_ref,
    pad_ref, tap_ref, prod_ref,
):
    strip = now0.shape[0]
    tokens = 4 * strip
    width = w_ref.shape[0]
    me = me_ref[0]
    pad_ref[:, :cols, :] = jnp.zeros((3, cols, 256), BF16)
    pad_ref[:, cols + tokens :, :] = jnp.zeros((3, cols, 256), BF16)
    for k, (now, old) in enumerate(((now0, old0), (now1, old1), (now2, old2), (now3, old3))):
        place = pl.ds(pl.multiple_of(cols + (me ^ k) * strip, 16), strip)
        pad_ref[2, place, :] = now[...]
        pad_ref[0, place, :] = old[0]
        place = pl.ds(pl.multiple_of(cols + (me ^ k ^ 2) * strip, 16), strip)
        pad_ref[1, place, :] = old[1]
    half = tokens // 2
    res_ref[...] = pad_ref[2, pl.ds(pl.multiple_of(cols + (me & 1) * half, 16), half), :]
    for tap in range(27):
        tap_ref[tap // 3, tap % 3 * width : (tap % 3 + 1) * width, :] = w_ref[
            :, tap * 256 : (tap + 1) * 256
        ]
    prod_ref[0:8, :] = jnp.zeros((8, 3 * width), F32)
    prod_ref[8 + tokens :, :] = jnp.zeros((8, 3 * width), F32)
    chunk = tokens // 4
    for part in range(4):
        total = jnp.zeros((chunk, 3 * width), F32)
        for tap in range(9):
            start = part * chunk + tap % 3 * cols
            total += dot_nt(pad_ref[tap // 3, start : start + chunk, :], tap_ref[tap])
        prod_ref[8 + part * chunk : 8 + (part + 1) * chunk, :] = total
    first = column_sum(prod_ref, tokens, cols, width)
    o_ref[...] = (first / (1.0 + jnp.exp(-first))).astype(BF16)


VMEM_SPEC = pl.BlockSpec(memory_space=pltpu.VMEM)
SMEM_SPEC = pl.BlockSpec(memory_space=pltpu.SMEM)


def first_conv(me, now, old, weight, cols):
    tokens = 4 * now[0].shape[0]
    width = weight.shape[0]

    def kernel(*refs):
        first_conv_kernel(cols, *refs)

    return pl.pallas_call(
        kernel,
        out_shape=(
            jax.ShapeDtypeStruct((tokens, width), BF16),
            jax.ShapeDtypeStruct((tokens // 2, 256), BF16),
        ),
        in_specs=[SMEM_SPEC] + [VMEM_SPEC] * 9,
        out_specs=(VMEM_SPEC, VMEM_SPEC),
        scratch_shapes=[
            pltpu.VMEM((3, tokens + 2 * cols, 256), BF16),
            pltpu.VMEM((9, 3 * width, 256), BF16),
            pltpu.VMEM((tokens + 16, 3 * width), F32),
        ],
        name="first_conv",
    )(me, *now, *old, weight)


def second_conv_kernel(
    cols, side_ref, a2_ref, a1_ref, a0_ref, w_ref, keep_ref, send_ref, pad_ref, tap_ref, prod_ref
):
    tokens, chans = a0_ref.shape
    depth = 3 * chans
    width = w_ref.shape[0]
    half = tokens // 2
    pad_ref[:cols, :] = jnp.zeros((cols, depth), BF16)
    pad_ref[cols + tokens :, :] = jnp.zeros((cols, depth), BF16)
    pad_ref[cols : cols + tokens, :] = jnp.concatenate(
        [a2_ref[...], a1_ref[...], a0_ref[...]], axis=1
    )
    for tap in range(9):
        tap_ref[tap // 3, tap % 3 * width : (tap % 3 + 1) * width, :] = w_ref[
            :, tap * depth : (tap + 1) * depth
        ]
    prod_ref[0:8, :] = jnp.zeros((8, 3 * width), F32)
    prod_ref[8 + tokens :, :] = jnp.zeros((8, 3 * width), F32)
    chunk = tokens // 4
    for part in range(4):
        total = jnp.zeros((chunk, 3 * width), F32)
        for tap in range(3):
            start = part * chunk + tap * cols
            total += dot_nt(pad_ref[start : start + chunk, :], tap_ref[tap])
        prod_ref[8 + part * chunk : 8 + (part + 1) * chunk, :] = total
    summed = column_sum(prod_ref, tokens, cols, width)

    @pl.when(side_ref[0] == 0)
    def _():
        keep_ref[...] = summed[:half]
        send_ref[...] = summed[half:].astype(BF16)

    @pl.when(side_ref[0] == 1)
    def _():
        keep_ref[...] = summed[half:]
        send_ref[...] = summed[:half].astype(BF16)


def second_conv(side, a2, a1, a0, weight, cols):
    tokens, chans = a0.shape
    width = weight.shape[0]

    def kernel(*refs):
        second_conv_kernel(cols, *refs)

    return pl.pallas_call(
        kernel,
        out_shape=(
            jax.ShapeDtypeStruct((tokens // 2, width), F32),
            jax.ShapeDtypeStruct((tokens // 2, width), BF16),
        ),
        in_specs=[SMEM_SPEC] + [VMEM_SPEC] * 4,
        out_specs=(VMEM_SPEC, VMEM_SPEC),
        scratch_shapes=[
            pltpu.VMEM((tokens + 2 * cols, 3 * chans), BF16),
            pltpu.VMEM((3, 3 * width, 3 * chans), BF16),
            pltpu.VMEM((tokens + 16, 3 * width), F32),
        ],
        name="second_conv",
    )(side, a2, a1, a0, weight)


def chip_sum_kernel(keep_ref, near_ref, o_ref):
    o_ref[...] = (keep_ref[...] + near_ref[...].astype(F32)).astype(BF16)


def chip_sum(keep, near):
    return pl.pallas_call(
        chip_sum_kernel,
        out_shape=jax.ShapeDtypeStruct(keep.shape, BF16),
        in_specs=[VMEM_SPEC] * 2,
        out_specs=VMEM_SPEC,
        name="chip_sum",
    )(keep, near)


def patch_kernel(cols, mine_ref, far_ref, res_ref, o_ref, whole_ref):
    chans = mine_ref.shape[1]
    rows = mine_ref.shape[0] // cols
    block = mine_ref[...].astype(F32) + far_ref[...].astype(F32) + res_ref[...].astype(F32)
    for part in range(chans // 128):
        whole_ref[part] = block[:, part * 128 : (part + 1) * 128]
    for p in range(rows // 2):
        for b in range(2):
            for e in range(2):
                for part in range(chans // 128):
                    lane = (b * 2 + e) * chans + part * 128
                    o_ref[p * cols // 2 : (p + 1) * cols // 2, lane : lane + 128] = whole_ref[
                        part, pl.ds((2 * p + b) * cols + e, cols // 2, stride=2), :
                    ].astype(BF16)


def patch_rows(mine, far, res, cols):
    tokens, chans = mine.shape

    def kernel(*refs):
        patch_kernel(cols, *refs)

    return pl.pallas_call(
        kernel,
        out_shape=jax.ShapeDtypeStruct((tokens // 4, 4 * chans), BF16),
        in_specs=[VMEM_SPEC] * 3,
        out_specs=VMEM_SPEC,
        scratch_shapes=[pltpu.VMEM((chans // 128, tokens, 128), F32)],
        name="patch_rows",
    )(mine, far, res)


def embed_kernel(me_ref, role_ref, mine_ref, near_ref, w0, w1, w2, w3, o_ref, all_ref):
    half = mine_ref.shape[0]
    width, depth = w0.shape
    core = me_ref[0] & 1
    for side, ref in ((core, mine_ref), (1 - core, near_ref)):
        all_ref[pl.ds(pl.multiple_of(side * half, 16), half), :] = ref[...]
    for start in range(0, width, 256):
        end = min(start + 256, width)
        total = None
        for k, w_ref in enumerate((w0, w1, w2, w3)):
            lanes = pl.ds(pl.multiple_of((role_ref[0] ^ k) * depth, depth), depth)
            part = dot_nt(all_ref[:, lanes], w_ref[start:end, :])
            total = part if total is None else total + part
        o_ref[:, start:end] = total.astype(BF16)


def embed_tokens(me, role, mine, near, weights):
    tokens = 2 * mine.shape[0]
    return pl.pallas_call(
        embed_kernel,
        out_shape=jax.ShapeDtypeStruct((tokens, weights[0].shape[0]), BF16),
        in_specs=[SMEM_SPEC] * 2 + [VMEM_SPEC] * 6,
        out_specs=VMEM_SPEC,
        scratch_shapes=[pltpu.VMEM((tokens, mine.shape[1]), BF16)],
        name="embed_tokens",
    )(me, role, mine, near, *weights)


def own_column(weight, index):
    return lax.dynamic_index_in_dim(weight.T, index, 0, keepdims=False)


def per_device(latent, conv_first, conv_second, embed_weight, qkv_weight):
    col_count = latent.shape[2]
    chan_count = latent.shape[3]
    lane_count = 4
    me = lax.axis_index("narrow")
    core = me % 2
    chans_here = chan_count // lane_count

    odd = lax.axis_index("wide") % NY == 1
    role = jnp.where(odd, me ^ 2, me)
    me_ref = me.astype(jnp.int32).reshape(1)

    mine = latent.reshape(-1, chan_count)
    far = other(mine, 2)
    near = other(mine, 1)
    cross = other(far, 1)
    old = jnp.stack([delayed(mine, 2), delayed(mine, 1)])
    old_far = other(old, 2)
    old_near = other(old, 1)
    old_cross = other(old_far, 1)

    pick = (
        lax.broadcasted_iota(jnp.int32, (chan_count, chans_here), 0)
        == lane_count * lax.broadcasted_iota(jnp.int32, (chan_count, chans_here), 1) + role
    ).astype(BF16)
    first_shard = own_column(conv_first, role).reshape(-1, 128)
    second_shard = jnp.dot(
        conv_second.T.reshape(-1, chan_count), pick, preferred_element_type=F32
    ).astype(BF16)
    second_shard = second_shard.reshape(lane_count, 3, 9, chans_here)
    second_shard = jnp.moveaxis(second_shard, 1, 2).reshape(-1, 128)
    quarter = embed_weight.shape[0] // 4
    embed_shard = lax.dynamic_slice_in_dim(embed_weight.T, role * quarter, quarter, axis=1)
    embed_shard = embed_shard.reshape(-1, 128)
    shards = jnp.concatenate([first_shard, second_shard, embed_shard])
    by_z = spread(shards, "wide", ALONG_Z)
    split = first_shard.shape[0]
    conv_weights = spread(by_z[:, : 2 * split], BOTH, ALONG_XY)
    conv_weights = in_wide_order(conv_weights, (2 * split, 128))
    first_weight = conv_weights[:, :split].reshape(chans_here, -1)
    second_weight = conv_weights[:, split:].reshape(chan_count, -1)
    embed_mine = spread(by_z[:, 2 * split :], BOTH, ALONG_XY)
    embed_mine = in_wide_order(embed_mine, embed_shard.shape).reshape(-1, quarter)
    embed_far = other(embed_mine, 2)
    embed_near = other(embed_mine, 1)
    embed_cross = other(embed_far, 1)

    activated, residual = first_conv(
        me_ref, (mine, near, far, cross), (old, old_near, old_far, old_cross),
        first_weight, col_count,
    )
    keep, send = second_conv(
        core.astype(jnp.int32).reshape(1),
        delayed(activated, 2),
        delayed(activated, 1),
        activated,
        second_weight,
        col_count,
    )
    summed = chip_sum(keep, other(send, 1))
    patches = patch_rows(summed, other(summed, 2), residual, col_count)
    embedded = embed_tokens(
        me_ref,
        role.astype(jnp.int32).reshape(1),
        patches,
        other(patches, 1),
        (embed_mine, embed_near, embed_far, embed_cross),
    )

    heads_here = qkv_weight.shape[2] // HEAD_DIM
    token_count = embedded.shape[0]
    key_raw = jnp.dot(embedded, qkv_weight[1], preferred_element_type=F32).astype(BF16).astype(F32)
    val_rows = jnp.dot(embedded, qkv_weight[2], preferred_element_type=F32).astype(BF16)
    query_raw = (
        jnp.dot(embedded, qkv_weight[0], preferred_element_type=F32).astype(BF16).astype(F32)
    )
    query_feat = (
        (jax.nn.elu(query_raw) + 1.0).astype(BF16).reshape(token_count, heads_here, HEAD_DIM)
    )
    key_feat = (jax.nn.elu(key_raw) + 1.0).astype(BF16).reshape(token_count, heads_here, HEAD_DIM)
    val_heads = val_rows.reshape(token_count, heads_here, HEAD_DIM)
    scores = jnp.einsum("thd,shd->hts", query_feat, key_feat, preferred_element_type=F32)
    row_ids = lax.broadcasted_iota(jnp.int32, (token_count, token_count), 0)
    col_ids = lax.broadcasted_iota(jnp.int32, (token_count, token_count), 1)
    scores = jnp.where((col_ids <= row_ids)[None], scores, 0.0)
    local_den = jnp.sum(scores, axis=-1)
    local_num = jnp.einsum(
        "hts,she->the", scores.astype(BF16), val_heads, preferred_element_type=F32
    )
    state_local = jnp.einsum("thd,the->hde", key_feat, val_heads, preferred_element_type=F32)
    key_local = jnp.sum(key_feat, axis=0, dtype=F32)
    flat_state = jnp.concatenate(
        [state_local.astype(BF16).reshape(-1), key_local.astype(BF16).reshape(-1)]
    )
    length_all = flat_state.shape[0]
    peer_count = lax.axis_size("wide")
    per_peer = -(-length_all // (peer_count * 1024)) * 1024
    piece_grid = jnp.pad(flat_state, (0, per_peer * peer_count - length_all)).reshape(
        peer_count, per_peer // 128, 128
    )
    lower_ones = (
        lax.broadcasted_iota(jnp.int32, (peer_count, peer_count), 1)
        < lax.broadcasted_iota(jnp.int32, (peer_count, peer_count), 0)
    ).astype(BF16)
    arrived = lax.all_to_all(piece_grid, "wide", split_axis=0, concat_axis=0, tiled=True)
    partial_sums = jnp.einsum("fg,grl->frl", lower_ones, arrived, preferred_element_type=F32)
    spread_back = lax.all_to_all(
        partial_sums.astype(BF16), "wide", split_axis=0, concat_axis=0, tiled=True
    )
    flat_prefix = spread_back.reshape(-1)[:length_all]
    state_size = state_local.size
    state_prev = flat_prefix[:state_size].reshape(state_local.shape)
    key_prev = flat_prefix[state_size:].reshape(key_local.shape)
    carried_num = jnp.einsum(
        "thd,hde->the", query_feat, state_prev, preferred_element_type=F32
    )
    carried_den = jnp.einsum("thd,hd->th", query_feat, key_prev, preferred_element_type=F32)
    result = (local_num + carried_num) / (local_den.T + carried_den)[..., None]
    return result.astype(BF16).reshape(token_count, heads_here * HEAD_DIM)


def solution(mesh):
    return jax.shard_map(
        per_device,
        mesh=mesh,
        in_specs=(
            P("wide", "narrow", None, None),
            P(None, "wide"),
            P(None, "wide"),
            P(None, "wide"),
            P(None, None, "narrow"),
        ),
        out_specs=P("wide", "narrow"),
        check_vma=False,
    )
```
